32 devices in a mesh: rep: 2 (over x), idx: 16 (over z, y, core).
Axes of the slice: x: 2, y: 2, z: 4, core: 2. Of those that a mesh axis runs over, the one named last changes fastest.
Arguments:
- images: bfloat16 [16448, 1408], P(('rep', 'idx')), parts along dimension 0, may hold values from -6 to 6
- norm_gain: float32 [1408], replicated, may hold values from 0.25 to 1.75
- qkv_values: bfloat16 [1408, 4224], P(None, 'idx'), may hold values from -0.5 to 0.5
- qkv_exponents: int32 [11, 4224], replicated, may hold values from -2 to 2
- proj_values: bfloat16 [1408, 1408], P(None, 'idx'), may hold values from -0.078125 to 0.078125
- proj_exponents: int32 [11, 1408], replicated, may hold values from -2 to 2
- captions: bfloat16 [32768, 1408], P(('rep', 'idx')), parts along dimension 0, may hold values from -0.15625 to 0.15625
- owners: int32 [16448, 1], P(('rep', 'idx')), parts along dimension 0, may hold values from 0 to 15; in each aligned block of 514 rows (0 to 513, 514 to 1027, ...) at most 34 rows name the same one
- candidates: int32 [16448, 4], P(('rep', 'idx')), parts along dimension 0, may hold values from 0 to 7, all different within a row
Outputs:
- embedding: bfloat16 [16448, 1408], P(('rep', 'idx')), parts along dimension 0
- scores: bfloat16 [16448, 4, 128], P(('rep', 'idx')), parts along dimension 0
The draws below stay inside these ranges and needn't reach their ends.
There are 2 independent parts, one for each index of `rep`. The reference program is written for one: setup_inputs(seed, part) draws one part's arguments, and reference() takes and returns one part's arrays. A program takes and returns all parts, laid end to end along the dimension named above; an argument that names none is the same for every part. Nothing has to cross between parts.
Inputs may be any that keep to these rules, and one draw needn't show every extreme that they name: `owners`: among the tokens of one device no owner is named more than 34 times, a bound that some block reaches. `candidates`: each token names 4 different caption blocks.
All inputs are finite; a program needn't handle non-finite values.
Results may differ from the reference program's by a relative error of at most 0.004.
The reference program's roundings to bfloat16 on the way (of `normed`, `w_qkv`, `w_proj`, `qkv_rows`, `attn_probs` and `mixed_heads`) count: a program that leaves them out, or rounds other values in their place, can miss the bound.
Values may be sent and summed in bfloat16 or wider, within the bound.
A program may use at most 192 MiB of HBM per device.

```python
import math
import jax
import jax.numpy as jnp
import numpy as np
from jax import lax

D = 1408
HEADS = 16
PATCHES = 257
QBLK = 128
CBLK = 8
CAPT = 128
K = 4
TOK_DEV = 514
TOKENS = 8224
CAP = 34
CAPTIONS = 16384
N_IDX = 16


def draw_qkv_values(key, part):
    base_draw = jax.random.normal(jax.random.fold_in(key, 11), (D, 3 * D), jnp.float32) * (D * 4.26) ** (-0.5)
    return jnp.clip(base_draw, -0.5, 0.5).astype(jnp.bfloat16)


def place_ends(drawn, rng, low, largest):
    index_at = [jax.random.randint(jax.random.fold_in(rng, axis), (), 0, length) for axis, length in enumerate(drawn.shape)]
    main_axis = drawn.shape.index(max(drawn.shape))
    neighbour = index_at[:main_axis] + [(index_at[main_axis] + 1) % drawn.shape[main_axis]] + index_at[main_axis + 1:]
    return drawn.at[tuple(index_at)].set(low).at[tuple(neighbour)].set(largest)


def steps_of(rng, shape, pieces, low, top_value):
    loudness, own = 1.0, jax.random.fold_in(rng, 6)
    for dim, shards_of in pieces:
        steps = jnp.exp(jax.random.uniform(jax.random.fold_in(own, dim), (shards_of,), jnp.float32, low / len(pieces), top_value / len(pieces)))
        loudness = loudness * jnp.repeat(steps, shape[dim] // shards_of).reshape([-1 if axis == dim else 1 for axis in range(len(shape))])
    return loudness


def distinct(rng, rows, amount, top, lift):
    order = jax.random.permutation(jax.random.fold_in(rng, 1), amount)
    boost = order
    for power in range(3):
        boost = boost * boost // amount
    boost = boost * lift // amount
    tickets = jax.random.randint(jax.random.fold_in(rng, 2), (rows, amount), 0, 4096) + boost
    sure = jax.random.permutation(jax.random.fold_in(rng, 3), rows)[jnp.arange(amount) % rows]
    tickets = jnp.where(jnp.arange(rows)[:, None] == sure[None, :], 1 << 14, tickets)
    score = tickets * amount + jnp.arange(amount)
    return lax.top_k(score.astype(jnp.int32), top)[1].astype(jnp.int32)


def routed_block(key, own, number, rows, number_of, top, limit, lean):
    sequence = jax.random.permutation(key, number_of)
    packed, ordinary = portions_of(number_of, rows * top, limit, lean, True), portions_of(number_of, rows * top, limit, lean, False)
    places = jnp.arange(number_of)

    def named(lengths, rotation):
        used = int((lengths > 0).sum())
        fixed = max(1, used // 4)
        passed = fixed + (places - fixed + rotation * (used - fixed)) % max(1, number_of - fixed)
        return jnp.zeros((number_of,), jnp.int32).at[sequence[jnp.where(places < fixed, places, passed)]].set(jnp.asarray(lengths, jnp.int32))

    lengths = jnp.where(number % 4 == 0, named(packed, number // 4), named(ordinary, number - number // 4 - 1))
    mixed = jax.random.permutation(jax.random.fold_in(own, 3), number_of)
    donor, sink = mixed[0:number_of // 2 * 2:2], mixed[1:number_of // 2 * 2:2]
    room = jnp.minimum(lengths[donor] - 1, limit - lengths[sink]) // 2
    room = jnp.where((donor == sequence[0]) | (sink == sequence[0]) | (lengths[sink] == 0), 0, jnp.maximum(room, 0))
    passed = jax.random.randint(jax.random.fold_in(own, 4), (number_of // 2,), 0, 1 << 20) % (room + 1)
    lengths = lengths.at[donor].add(-passed).at[sink].add(passed)
    items = jnp.searchsorted(jnp.cumsum(lengths), jnp.arange(rows * top), side="right").astype(jnp.int32)
    grid = items.reshape(top, rows).T
    grid = grid[jax.random.permutation(jax.random.fold_in(own, 1), rows)]
    rotation = jax.random.randint(jax.random.fold_in(own, 2), (rows, 1), 0, top)
    return jnp.take_along_axis(grid, (jnp.arange(top)[None, :] + rotation) % top, axis=1)


def portions_of(amount, total, most, lean, full):
    loads = [(1 << 20) // math.isqrt(standing ** lean) + 1 for standing in range(1, amount + 1)]
    largest = most if full else min(most, max(-(-total // amount), total * loads[0] // sum(loads)))
    least = 1 if total - largest >= amount - 1 else 0
    holding, rest = [largest] + [least] * (amount - 1), total - largest - least * (amount - 1)
    while rest > 0:
        free = [i for i in range(1, amount) if holding[i] < largest] or [i for i in range(1, amount) if holding[i] < most]
        whole, budget = sum([loads[i] for i in free]), rest
        for i in free:
            addition = min(most - holding[i], max(1, budget * loads[i] // whole), rest)
            holding[i] = holding[i] + addition
            rest = rest - addition
    return np.array(holding)


def normal_values(rng, shape, scale, bound, split=(), kind=jnp.bfloat16):
    level = steps_of(rng, shape, split, -0.22, 0.18) if split else 1.0
    entries = jax.random.normal(rng, shape, jnp.float32) * scale * level
    return jnp.minimum(jnp.maximum(entries, -bound), bound).astype(kind)


def setup_inputs(seed: int = 0, part: int = 0) -> dict:
    streams_of = jax.random.split(jax.random.key(seed), 10)
    own_keys = jax.random.split(jax.random.fold_in(streams_of[9], part), 10)
    images = normal_values(own_keys[0], (TOKENS, D), 1.0, 6.0, ((0, 16),))
    norm_gain = jnp.clip(1.0 + 0.15 * jax.random.normal(streams_of[1], (D,), jnp.float32), 0.25, 1.75)
    qkv_values = draw_qkv_values(jax.random.fold_in(streams_of[9], 71), part)
    qkv_exponents = place_ends(jax.random.randint(streams_of[3], (D // QBLK, 3 * D), -2, 3), jax.random.fold_in(streams_of[3], 1), -2, 2).astype(jnp.int32)
    proj_values = normal_values(streams_of[4], (D, D), (4 * D) ** -0.5, 0.078125, ((1, 16),))
    proj_exponents = place_ends(jax.random.randint(streams_of[5], (D // QBLK, D), -2, 3), jax.random.fold_in(streams_of[5], 1), -2, 2).astype(jnp.int32)
    captions = normal_values(own_keys[6], (CAPTIONS, D), D ** -0.5, 0.15625, ((0, 16),))
    owners_keys = jax.random.split(jax.random.fold_in(own_keys[7], 1), TOKENS // TOK_DEV)
    owners_turns = jax.random.permutation(jax.random.fold_in(own_keys[7], 3), TOKENS // TOK_DEV)
    owners = jax.vmap(lambda own, number: routed_block(jax.random.fold_in(own_keys[7], 2), own, number, TOK_DEV, N_IDX, 1, CAP, 2))(owners_keys, owners_turns).reshape((TOKENS, 1))
    candidates = distinct(own_keys[8], TOKENS, CBLK, K, 4096)
    return dict(images=images, norm_gain=norm_gain, qkv_values=qkv_values, qkv_exponents=qkv_exponents, proj_values=proj_values, proj_exponents=proj_exponents, captions=captions, owners=owners, candidates=candidates)


def dequant(stored, exponents):
    row_count, col_count = stored.shape
    block_count = exponents.shape[0]
    scaled = stored.astype(jnp.float32).reshape(block_count, row_count // block_count, col_count)
    scaled = scaled * jnp.exp2(exponents.astype(jnp.float32))[:, None, :]
    return scaled.reshape(row_count, col_count).astype(jnp.bfloat16)

def layer_norm(token_rows, norm_gain):
    values = token_rows.astype(jnp.float32)
    centered = values - lax.optimization_barrier(jnp.mean(values, axis=-1, keepdims=True))
    inv_scale = lax.rsqrt(lax.optimization_barrier(jnp.mean(centered * centered, axis=-1, keepdims=True)) + 1e-06)
    return (centered * inv_scale * norm_gain.astype(jnp.float32)).astype(jnp.bfloat16)

def attend(qkv_rows):
    head_dim = D // HEADS
    grouped = qkv_rows.reshape(-1, PATCHES, 3, HEADS, head_dim).astype(jnp.float32)
    queries = grouped[:, :, 0]
    keys_all = grouped[:, :, 1]
    values_all = grouped[:, :, 2]
    logits = jnp.einsum('gqhd,gkhd->ghqk', queries, keys_all) * head_dim ** (-0.5)
    logits = logits - lax.optimization_barrier(jnp.max(logits, axis=-1, keepdims=True))
    weights = jnp.exp(logits)
    attn_probs = (weights / lax.optimization_barrier(jnp.sum(weights, axis=-1, keepdims=True))).astype(jnp.bfloat16)
    mixed_heads = jnp.einsum('ghqk,gkhd->gqhd', attn_probs.astype(jnp.float32), values_all)
    return mixed_heads.astype(jnp.bfloat16).reshape(-1, D)

def reference(images, norm_gain, qkv_values, qkv_exponents, proj_values, proj_exponents, captions, owners, candidates):
    w_qkv = dequant(qkv_values, qkv_exponents)
    w_proj = dequant(proj_values, proj_exponents)

    def layer_pass(token_rows):
        normed = layer_norm(token_rows, norm_gain)
        qkv_rows = jnp.dot(normed, w_qkv, preferred_element_type=jnp.float32).astype(jnp.bfloat16)
        mixed_heads = attend(qkv_rows)
        hidden = token_rows.astype(jnp.float32) + jnp.dot(mixed_heads, w_proj, preferred_element_type=jnp.float32)
        inv_scale = lax.rsqrt(lax.optimization_barrier(jnp.mean(hidden * hidden, axis=-1, keepdims=True)) + 1e-06)
        return (hidden * inv_scale).astype(jnp.bfloat16)
    embedding = lax.map(layer_pass, images.reshape(-1, PATCHES, D)).reshape(-1, D)
    blocks = captions.reshape(-1, CAPT, D)
    chosen = (owners[:, 0:1] * CBLK + candidates).astype(jnp.int32)

    def score_block(block_pair):
        token_rows, block_picks = block_pair
        picked = blocks[block_picks].astype(jnp.float32)
        return jnp.einsum('bd,bkjd->bkj', token_rows.astype(jnp.float32), picked).astype(jnp.bfloat16)
    scores = lax.map(score_block, (embedding.reshape(-1, 16, D), chosen.reshape(-1, 16, K)))
    return (embedding, scores.reshape(-1, K, CAPT))
```

```python
import functools
import jax
import jax.numpy as jnp
from jax import lax
from jax.experimental import pallas as pl
from jax.experimental.pallas import tpu as pltpu
from jax.sharding import PartitionSpec as P

HEADS = 16
PATCHES = 257
CBLK = 8
CAPT = 128
F32 = jnp.float32
BF16 = jnp.bfloat16
VMEM = pltpu.VMEM
VLIMIT = 60 * 1024 * 1024


def dequant_rows(stored, exponents):
    row_count, col_count = stored.shape
    block_count = exponents.shape[0]
    turned = stored.T.astype(F32).reshape(col_count, block_count, row_count // block_count)
    scaled = turned * jnp.exp2(exponents.astype(F32)).T[:, :, None]
    return scaled.reshape(col_count, row_count).astype(BF16)


def layer_norm(token_rows, norm_gain):
    values = token_rows.astype(F32)
    centered = values - jnp.mean(values, axis=-1, keepdims=True)
    inv_scale = lax.rsqrt(jnp.mean(centered * centered, axis=-1, keepdims=True) + 1e-06)
    return (centered * inv_scale * norm_gain).astype(BF16)


def dot_nt(left, right):
    return lax.dot_general(left, right, (((1,), (1,)), ((), ())), preferred_element_type=F32)


def qkv_kernel(images_ref, gain_ref, w_ref, out_ref, normed):
    group, unit, head_dim = out_ref.shape[0], out_ref.shape[1], out_ref.shape[2]

    @pl.when(pl.program_id(0) == 0)
    def _():
        for g in range(group):
            normed[g] = layer_norm(images_ref[g], gain_ref[...])

    for g in range(group):
        rows = dot_nt(w_ref[...], normed[g])
        out_ref[g] = rows.reshape(unit, head_dim, rows.shape[1]).astype(BF16)


def qkv_call(images3, gain, w_rows):
    group, patches, width = images3.shape
    head_dim = width // HEADS
    units = w_rows.shape[0] // head_dim
    step = 4
    return pl.pallas_call(
        qkv_kernel,
        grid=(units // step,),
        in_specs=[
            pl.BlockSpec((group, patches, width), lambda i: (0, 0, 0)),
            pl.BlockSpec((1, width), lambda i: (0, 0)),
            pl.BlockSpec((step * head_dim, width), lambda i: (i, 0)),
        ],
        out_specs=pl.BlockSpec((group, step, head_dim, patches), lambda i: (0, i, 0, 0)),
        out_shape=jax.ShapeDtypeStruct((group, units, head_dim, patches), BF16),
        scratch_shapes=[pltpu.VMEM((group, patches, width), BF16)],
        compiler_params=pltpu.CompilerParams(vmem_limit_bytes=VLIMIT),
        name="qkv",
    )(images3, gain, w_rows)


def attend_kernel(qkv_ref, proj_ref, images_ref, slot_ref, emb_ref, send_ref, mixed):
    group, units, head_dim, patches = qkv_ref.shape
    width = HEADS * head_dim
    scale = head_dim ** (-0.5)
    for g in range(group):

        @pl.loop(0, HEADS)
        def _(h):
            queries, keys, vals = qkv_ref[g, h], qkv_ref[g, HEADS + h], qkv_ref[g, 2 * HEADS + h]
            logits = lax.dot_general(
                keys, queries, (((0,), (0,)), ((), ())), preferred_element_type=F32
            )
            logits = logits * scale
            weights = jnp.exp(logits - jnp.max(logits, axis=0, keepdims=True))
            probs = weights * (1.0 / jnp.sum(weights, axis=0, keepdims=True))
            out = jnp.dot(vals, probs.astype(BF16), preferred_element_type=F32)
            mixed[pl.ds(pl.multiple_of(h * head_dim, 8), head_dim), :] = out

        left = mixed[...].T.astype(BF16)
        hidden = images_ref[g].astype(F32) + dot_nt(left, proj_ref[...])
        inv_scale = lax.rsqrt(jnp.mean(hidden * hidden, axis=-1, keepdims=True) + 1e-06)
        emb_ref[g * patches:(g + 1) * patches, :] = (hidden * inv_scale).astype(BF16)
    slots = send_ref.shape[0]
    tokens = group * patches
    pick = lax.broadcasted_iota(jnp.int32, (slots, tokens), 0) == slot_ref[...]
    onehot = jnp.where(pick, 1.0, 0.0).astype(BF16)
    send_ref[...] = jnp.dot(onehot, emb_ref[...], preferred_element_type=F32).astype(BF16)


def attend_call(qkv, w_proj, images3, slot_row, slots):
    group, patches, width = images3.shape
    full = pl.BlockSpec(memory_space=VMEM)
    return pl.pallas_call(
        attend_kernel,
        in_specs=[full] * 4,
        out_specs=(full, full),
        out_shape=(
            jax.ShapeDtypeStruct((group * patches, width), BF16),
            jax.ShapeDtypeStruct((slots, width), BF16),
        ),
        scratch_shapes=[pltpu.VMEM((width, patches), F32)],
        compiler_params=pltpu.CompilerParams(vmem_limit_bytes=VLIMIT),
        name="attend",
    )(qkv, w_proj, images3, slot_row)


def score_kernel(rows_ref, picks_ref, captions_ref, out_ref):
    every = dot_nt(rows_ref[...], captions_ref[...]).astype(BF16)
    for k in range(picks_ref.shape[1]):
        pick = picks_ref[:, k:k + 1].astype(F32)
        chosen = jnp.zeros((every.shape[0], CAPT), F32)
        for b in range(CBLK):
            block = every[:, b * CAPT:(b + 1) * CAPT].astype(F32)
            chosen = jnp.where(pick == float(b), block, chosen)
        out_ref[:, k * CAPT:(k + 1) * CAPT] = chosen.astype(BF16)


def score_call(rows, picks, captions):
    full = pl.BlockSpec(memory_space=VMEM)
    return pl.pallas_call(
        score_kernel,
        in_specs=[full] * 3,
        out_specs=full,
        out_shape=jax.ShapeDtypeStruct((rows.shape[0], picks.shape[1] * CAPT), BF16),
        compiler_params=pltpu.CompilerParams(vmem_limit_bytes=VLIMIT),
        name="score",
    )(rows, picks, captions)


def return_kernel(slot_ref, rows_ref, out_ref):
    tokens, slots = out_ref.shape[0], rows_ref.shape[0]
    pick = lax.broadcasted_iota(jnp.int32, (tokens, slots), 1) == slot_ref[...]
    onehot = jnp.where(pick, 1.0, 0.0).astype(BF16)
    got = jnp.dot(onehot, rows_ref[...], preferred_element_type=F32).astype(BF16)
    for k in range(out_ref.shape[1]):
        out_ref[:, k, :] = got[:, k * CAPT:(k + 1) * CAPT]


def return_call(slot_col, rows, pick_count):
    full = pl.BlockSpec(memory_space=VMEM)
    return pl.pallas_call(
        return_kernel,
        in_specs=[full] * 2,
        out_specs=full,
        out_shape=jax.ShapeDtypeStruct((slot_col.shape[0], pick_count, CAPT), BF16),
        compiler_params=pltpu.CompilerParams(vmem_limit_bytes=VLIMIT),
        name="give_back",
    )(slot_col, rows)


def local(
    images,
    norm_gain,
    qkv_values,
    qkv_exponents,
    proj_values,
    proj_exponents,
    captions,
    owners,
    candidates,
):
    token_count, width = images.shape
    peer_count = lax.axis_size("idx")
    me = lax.axis_index("idx")
    capacity = (token_count + peer_count - 1) // peer_count + 1

    def own_exponents(exponents, cols):
        return lax.dynamic_slice_in_dim(exponents, me * cols, cols, axis=1)

    qkv_cols, proj_cols = qkv_values.shape[1], proj_values.shape[1]
    qkv_own = dequant_rows(qkv_values, own_exponents(qkv_exponents, qkv_cols))
    proj_own = dequant_rows(proj_values, own_exponents(proj_exponents, proj_cols))
    w_qkv = lax.all_gather(qkv_own, "idx", axis=0, tiled=True)
    w_proj = lax.all_gather(proj_own, "idx", axis=0, tiled=True)

    owner_ids = owners[:, 0]
    onehot = (owner_ids[:, None] == jnp.arange(peer_count, dtype=jnp.int32)[None, :]).astype(
        jnp.int32
    )
    slot_rank = jnp.sum((jnp.cumsum(onehot, axis=0) - onehot) * onehot, axis=1)
    slot_index = owner_ids * capacity + slot_rank
    slots = peer_count * capacity
    pick_count = candidates.shape[1]
    dispatch = (jnp.arange(slots, dtype=jnp.int32)[:, None] == slot_index[None, :]).astype(BF16)
    send_picks = jnp.dot(dispatch, candidates.astype(BF16), preferred_element_type=F32).astype(BF16)
    got_picks = lax.all_to_all(
        send_picks.reshape(peer_count, capacity, pick_count), "idx", split_axis=0, concat_axis=0, tiled=True
    ).reshape(slots, pick_count)

    images3 = images.reshape(-1, PATCHES, width)
    qkv = qkv_call(images3, norm_gain[None, :], w_qkv)
    embedding, send_rows = attend_call(qkv, w_proj, images3, slot_index[None, :], slots)
    arrived = lax.all_to_all(
        send_rows.reshape(peer_count, capacity, width), "idx", split_axis=0, concat_axis=0, tiled=True
    ).reshape(slots, width)
    chosen = score_call(arrived, got_picks, captions)
    returned = lax.all_to_all(
        chosen.reshape(peer_count, capacity, pick_count * CAPT), "idx", split_axis=0, concat_axis=0, tiled=True
    ).reshape(slots, pick_count * CAPT)
    scores = return_call(slot_index[:, None], returned, pick_count)
    return (embedding, scores)


def solution(mesh):
    placed = (
        P(("rep", "idx"), None),
        P(),
        P(None, "idx"),
        P(),
        P(None, "idx"),
        P(),
        P(("rep", "idx"), None),
        P(("rep", "idx"), None),
        P(("rep", "idx"), None),
    )
    return jax.shard_map(
        local,
        mesh=mesh,
        in_specs=placed,
        out_specs=(P(("rep", "idx"), None), P(("rep", "idx"), None, None)),
        check_vma=False,
    )
```

```python
import functools
import jax
import jax.numpy as jnp
from jax import lax
from jax.experimental import pallas as pl
from jax.experimental.pallas import tpu as pltpu
from jax.sharding import PartitionSpec as P

HEADS = 16
PATCHES = 257
CBLK = 8
CAPT = 128
F32 = jnp.float32
BF16 = jnp.bfloat16
VMEM = pltpu.VMEM
VLIMIT = 60 * 1024 * 1024


def dequant_rows(stored, exponents):
    row_count, col_count = stored.shape
    block_count = exponents.shape[0]
    turned = stored.T.astype(F32).reshape(col_count, block_count, row_count // block_count)
    scaled = turned * jnp.exp2(exponents.astype(F32)).T[:, :, None]
    return scaled.reshape(col_count, row_count).astype(BF16)


def layer_norm(token_rows, norm_gain):
    values = token_rows.astype(F32)
    centered = values - jnp.mean(values, axis=-1, keepdims=True)
    inv_scale = lax.rsqrt(jnp.mean(centered * centered, axis=-1, keepdims=True) + 1e-06)
    return (centered * inv_scale * norm_gain).astype(BF16)


def dot_nt(left, right):
    return lax.dot_general(left, right, (((1,), (1,)), ((), ())), preferred_element_type=F32)


MESH = pl.DeviceIdType.MESH
SHARE = 11


def gather_kernel(q_own, p_own, q_out, p_out, q_hold, p_hold, rz, ry, rx, rc, sz, sy, sx, sc, held):
    peers = q_out.shape[0]
    nz = peers // 4
    me = lax.axis_index("idx")
    x = lax.axis_index("rep")
    z, y, c = me // 4, (me // 2) % 2, me % 2
    own, out = (q_own, p_own), (q_out, p_out)

    def at(zz, yy, cc):
        return (zz * 2 + yy) * 2 + cc

    to_y, to_c, to_x = (x, at(z, 1 - y, c)), (x, at(z, y, 1 - c)), (1 - x, me)
    to_up, to_down = (x, me + 4), (x, me - 4)

    barrier = pltpu.get_barrier_semaphore()

    def greet(target):
        pl.semaphore_signal(barrier, inc=1, device_id=target, device_id_type=MESH)

    for target in (to_y, to_c, to_x):
        greet(target)

    @pl.when(z + 1 < nz)
    def _():
        greet(to_up)

    @pl.when(z > 0)
    def _():
        greet(to_down)

    greeted = 3 + jnp.where(z + 1 < nz, 1, 0) + jnp.where(z > 0, 1, 0)
    pl.semaphore_wait(barrier, greeted)

    def rows(a, k):
        unit = own[a].shape[0] // SHARE
        if k == 0:
            return pl.ds(0, 3 * unit)
        if k == 3:
            return pl.ds(0, SHARE * unit)
        side = x if k == 1 else 1 - x
        return pl.ds(pl.multiple_of((3 + 4 * side) * unit, 8), 4 * unit)

    def copy(a, shard, k, mine, send, recv, target):
        span = rows(a, k)
        return pltpu.make_async_remote_copy(
            src_ref=own[a].at[span] if mine else out[a].at[shard, span],
            dst_ref=out[a].at[shard, span],
            send_sem=send,
            recv_sem=recv,
            device_id=target,
            device_id_type=MESH,
        )

    def pos(zz, yy):
        return zz * 2 + yy

    def up(a, zz, k, mine=False):
        return copy(a, at(zz, y, c), k, mine, sz.at[0, a, zz, k], rz.at[a, zz, k], to_up)

    def down(a, zz, k, mine=False):
        return copy(a, at(zz, y, c), k, mine, sz.at[1, a, zz, k], rz.at[a, zz, k], to_down)

    def across(a, zz, k, yy, mine=False):
        return copy(a, at(zz, yy, c), k, mine, sy.at[a, zz, k], ry.at[a, zz, k], to_y)

    def plane(a, zz, yy, k):
        return copy(a, at(zz, yy, c), k, False, sx.at[a, pos(zz, yy)], rx.at[a, pos(zz, yy)], to_x)

    def core(a, zz, yy, cc, k, mine=False):
        slot = 0 if k == 3 else k
        return copy(
            a, at(zz, yy, cc), k, mine, sc.at[a, pos(zz, yy), slot], rc.at[a, pos(zz, yy), slot], to_c
        )

    def each(distance, body):
        if distance == 0:
            body(z, 0)
            return

        @pl.when(z - distance >= 0)
        def _():
            body(z - distance, -1)

        @pl.when(z + distance < nz)
        def _():
            body(z + distance, 1)

    holds = []
    for a in range(2):
        for k in (1, 0):

            @pl.when(z + 1 < nz)
            def _():
                up(a, z, k, True).start()

            @pl.when(z > 0)
            def _():
                down(a, z, k, True).start()

            across(a, z, k, y, True).start()
        core(a, z, y, c, 3, True).start()
        hold = (q_hold, p_hold)[a]
        load = pltpu.make_async_copy(own[a], hold, held.at[a, 0])
        load.start()
        holds.append((load, pltpu.make_async_copy(hold, out[a].at[me], held.at[a, 1])))
    for load, store in holds:
        load.wait()
        store.start()

    for a in range(2):
        for step in range(1, nz + 2):
            if step < nz:

                def from_chain(zz, side):
                    for k in (1, 0):
                        up(a, zz, k).wait_recv()
                        if side < 0:

                            @pl.when(z + 1 < nz)
                            def _():
                                up(a, zz, k).start()
                        else:

                            @pl.when(z > 0)
                            def _():
                                down(a, zz, k).start()

                        across(a, zz, k, y).start()
                        if k == 1:
                            plane(a, zz, y, 1).start()
                        core(a, zz, y, c, k).start()

                each(step, from_chain)
            if step <= nz:

                def from_across(zz, side):
                    for k in (1, 0):
                        across(a, zz, k, 1 - y).wait_recv()
                        if k == 1:
                            plane(a, zz, 1 - y, 1).start()
                        core(a, zz, 1 - y, c, k).start()

                each(step - 1, from_across)
            if step >= 2:

                def from_plane(zz, side):
                    if side != 0:
                        plane(a, zz, y, 2).wait_recv()
                        core(a, zz, y, c, 2).start()
                    plane(a, zz, 1 - y, 2).wait_recv()
                    core(a, zz, 1 - y, c, 2).start()

                each(step - 2, from_plane)

    for a in range(2):
        for distance in range(nz):

            def finish(zz, side):
                first = side == 0
                for k in (1, 0):
                    if side <= 0:

                        @pl.when(z + 1 < nz)
                        def _():
                            up(a, zz, k, first).wait_send()

                    if side >= 0:

                        @pl.when(z > 0)
                        def _():
                            down(a, zz, k, first).wait_send()

                    across(a, zz, k, y, first).wait_send()
                for yy, mine in ((y, first), (1 - y, False)):
                    if mine:
                        core(a, zz, yy, c, 3, True).wait_send()
                        core(a, zz, yy, 1 - c, 3).wait_recv()
                        continue
                    plane(a, zz, yy, 1).wait_send()
                    for k in (1, 0, 2):
                        core(a, zz, yy, c, k).wait_send()
                        core(a, zz, yy, 1 - c, k).wait_recv()

            each(distance, finish)
    for load, store in holds:
        store.wait()


def gather_call(q_own, p_own, peers):
    anywhere = pl.BlockSpec(memory_space=pl.ANY)
    nz = peers // 4
    dma = pltpu.SemaphoreType.DMA
    return pl.pallas_call(
        gather_kernel,
        in_specs=[anywhere] * 2,
        out_specs=(anywhere, anywhere),
        out_shape=tuple(jax.ShapeDtypeStruct((peers,) + own.shape, own.dtype) for own in (q_own, p_own)),
        scratch_shapes=[
            pltpu.VMEM(q_own.shape, q_own.dtype),
            pltpu.VMEM(p_own.shape, p_own.dtype),
            dma((2, nz, 2)),
            dma((2, nz, 2)),
            dma((2, 2 * nz)),
            dma((2, 2 * nz, 3)),
            dma((2, 2, nz, 2)),
            dma((2, nz, 2)),
            dma((2, 2 * nz)),
            dma((2, 2 * nz, 3)),
            dma((2, 2)),
        ],
        compiler_params=pltpu.CompilerParams(
            collective_id=0, has_side_effects=True, vmem_limit_bytes=4 * 1024 * 1024
        ),
        name="gather_weights",
    )(q_own, p_own)


def gather_rows(q_own, p_own, peers, reps):
    fits = all(own.shape[0] % (8 * SHARE) == 0 for own in (q_own, p_own))
    if fits and peers % 8 == 0 and reps == 2:
        w_qkv, w_proj = gather_call(q_own, p_own, peers)
        return tuple(w.reshape(-1, w.shape[2]) for w in (w_qkv, w_proj))
    return tuple(lax.all_gather(own, "idx", axis=0, tiled=True) for own in (q_own, p_own))


def qkv_kernel(images_ref, gain_ref, w_ref, out_ref, normed):
    group, unit, head_dim = out_ref.shape[0], out_ref.shape[1], out_ref.shape[2]

    @pl.when(pl.program_id(0) == 0)
    def _():
        for g in range(group):
            normed[g] = layer_norm(images_ref[g], gain_ref[...])

    for g in range(group):
        rows = dot_nt(w_ref[...], normed[g])
        out_ref[g] = rows.reshape(unit, head_dim, rows.shape[1]).astype(BF16)


def qkv_call(images3, gain, w_rows):
    group, patches, width = images3.shape
    head_dim = width // HEADS
    units = w_rows.shape[0] // head_dim
    step = 4
    return pl.pallas_call(
        qkv_kernel,
        grid=(units // step,),
        in_specs=[
            pl.BlockSpec((group, patches, width), lambda i: (0, 0, 0)),
            pl.BlockSpec((1, width), lambda i: (0, 0)),
            pl.BlockSpec((step * head_dim, width), lambda i: (i, 0)),
        ],
        out_specs=pl.BlockSpec((group, step, head_dim, patches), lambda i: (0, i, 0, 0)),
        out_shape=jax.ShapeDtypeStruct((group, units, head_dim, patches), BF16),
        scratch_shapes=[pltpu.VMEM((group, patches, width), BF16)],
        compiler_params=pltpu.CompilerParams(vmem_limit_bytes=VLIMIT),
        name="qkv",
    )(images3, gain, w_rows)


def attend_kernel(qkv_ref, proj_ref, images_ref, slot_ref, emb_ref, send_ref, mixed):
    group, units, head_dim, patches = qkv_ref.shape
    width = HEADS * head_dim
    scale = head_dim ** (-0.5)
    for g in range(group):

        @pl.loop(0, HEADS)
        def _(h):
            queries, keys, vals = qkv_ref[g, h], qkv_ref[g, HEADS + h], qkv_ref[g, 2 * HEADS + h]
            logits = lax.dot_general(
                keys, queries, (((0,), (0,)), ((), ())), preferred_element_type=F32
            )
            logits = logits * scale
            weights = jnp.exp(logits - jnp.max(logits, axis=0, keepdims=True))
            probs = weights * (1.0 / jnp.sum(weights, axis=0, keepdims=True))
            out = jnp.dot(vals, probs.astype(BF16), preferred_element_type=F32)
            mixed[pl.ds(pl.multiple_of(h * head_dim, 8), head_dim), :] = out

        left = mixed[...].T.astype(BF16)
        hidden = images_ref[g].astype(F32) + dot_nt(left, proj_ref[...])
        inv_scale = lax.rsqrt(jnp.mean(hidden * hidden, axis=-1, keepdims=True) + 1e-06)
        emb_ref[g * patches:(g + 1) * patches, :] = (hidden * inv_scale).astype(BF16)
    slots = send_ref.shape[0]
    tokens = group * patches
    pick = lax.broadcasted_iota(jnp.int32, (slots, tokens), 0) == slot_ref[...]
    onehot = jnp.where(pick, 1.0, 0.0).astype(BF16)
    send_ref[...] = jnp.dot(onehot, emb_ref[...], preferred_element_type=F32).astype(BF16)


def attend_call(qkv, w_proj, images3, slot_row, slots):
    group, patches, width = images3.shape
    full = pl.BlockSpec(memory_space=VMEM)
    return pl.pallas_call(
        attend_kernel,
        in_specs=[full] * 4,
        out_specs=(full, full),
        out_shape=(
            jax.ShapeDtypeStruct((group * patches, width), BF16),
            jax.ShapeDtypeStruct((slots, width), BF16),
        ),
        scratch_shapes=[pltpu.VMEM((width, patches), F32)],
        compiler_params=pltpu.CompilerParams(vmem_limit_bytes=VLIMIT),
        name="attend",
    )(qkv, w_proj, images3, slot_row)


def score_kernel(rows_ref, picks_ref, captions_ref, out_ref):
    every = dot_nt(rows_ref[...], captions_ref[...]).astype(BF16)
    for k in range(picks_ref.shape[1]):
        pick = picks_ref[:, k:k + 1].astype(F32)
        chosen = jnp.zeros((every.shape[0], CAPT), F32)
        for b in range(CBLK):
            block = every[:, b * CAPT:(b + 1) * CAPT].astype(F32)
            chosen = jnp.where(pick == float(b), block, chosen)
        out_ref[:, k * CAPT:(k + 1) * CAPT] = chosen.astype(BF16)


def score_call(rows, picks, captions):
    full = pl.BlockSpec(memory_space=VMEM)
    return pl.pallas_call(
        score_kernel,
        in_specs=[full] * 3,
        out_specs=full,
        out_shape=jax.ShapeDtypeStruct((rows.shape[0], picks.shape[1] * CAPT), BF16),
        compiler_params=pltpu.CompilerParams(vmem_limit_bytes=VLIMIT),
        name="score",
    )(rows, picks, captions)


def return_kernel(slot_ref, rows_ref, out_ref):
    tokens, slots = out_ref.shape[0], rows_ref.shape[0]
    pick = lax.broadcasted_iota(jnp.int32, (tokens, slots), 1) == slot_ref[...]
    onehot = jnp.where(pick, 1.0, 0.0).astype(BF16)
    got = jnp.dot(onehot, rows_ref[...], preferred_element_type=F32).astype(BF16)
    for k in range(out_ref.shape[1]):
        out_ref[:, k, :] = got[:, k * CAPT:(k + 1) * CAPT]


def return_call(slot_col, rows, pick_count):
    full = pl.BlockSpec(memory_space=VMEM)
    return pl.pallas_call(
        return_kernel,
        in_specs=[full] * 2,
        out_specs=full,
        out_shape=jax.ShapeDtypeStruct((slot_col.shape[0], pick_count, CAPT), BF16),
        compiler_params=pltpu.CompilerParams(vmem_limit_bytes=VLIMIT),
        name="give_back",
    )(slot_col, rows)


def local(
    images,
    norm_gain,
    qkv_values,
    qkv_exponents,
    proj_values,
    proj_exponents,
    captions,
    owners,
    candidates,
):
    token_count, width = images.shape
    peer_count = lax.axis_size("idx")
    me = lax.axis_index("idx")
    capacity = (token_count + peer_count - 1) // peer_count + 1

    def own_exponents(exponents, cols):
        return lax.dynamic_slice_in_dim(exponents, me * cols, cols, axis=1)

    qkv_cols, proj_cols = qkv_values.shape[1], proj_values.shape[1]
    qkv_own = dequant_rows(qkv_values, own_exponents(qkv_exponents, qkv_cols))
    proj_own = dequant_rows(proj_values, own_exponents(proj_exponents, proj_cols))
    w_qkv, w_proj = gather_rows(qkv_own, proj_own, peer_count, lax.axis_size("rep"))

    owner_ids = owners[:, 0]
    onehot = (owner_ids[:, None] == jnp.arange(peer_count, dtype=jnp.int32)[None, :]).astype(
        jnp.int32
    )
    slot_rank = jnp.sum((jnp.cumsum(onehot, axis=0) - onehot) * onehot, axis=1)
    slot_index = owner_ids * capacity + slot_rank
    slots = peer_count * capacity
    pick_count = candidates.shape[1]
    dispatch = (jnp.arange(slots, dtype=jnp.int32)[:, None] == slot_index[None, :]).astype(BF16)
    send_picks = jnp.dot(dispatch, candidates.astype(BF16), preferred_element_type=F32).astype(BF16)
    got_picks = lax.all_to_all(
        send_picks.reshape(peer_count, capacity, pick_count), "idx", split_axis=0, concat_axis=0, tiled=True
    ).reshape(slots, pick_count)

    images3 = images.reshape(-1, PATCHES, width)
    qkv = qkv_call(images3, norm_gain[None, :], w_qkv)
    embedding, send_rows = attend_call(qkv, w_proj, images3, slot_index[None, :], slots)
    arrived = lax.all_to_all(
        send_rows.reshape(peer_count, capacity, width), "idx", split_axis=0, concat_axis=0, tiled=True
    ).reshape(slots, width)
    chosen = score_call(arrived, got_picks, captions)
    returned = lax.all_to_all(
        chosen.reshape(peer_count, capacity, pick_count * CAPT), "idx", split_axis=0, concat_axis=0, tiled=True
    ).reshape(slots, pick_count * CAPT)
    scores = return_call(slot_index[:, None], returned, pick_count)
    return (embedding, scores)


def solution(mesh):
    placed = (
        P(("rep", "idx"), None),
        P(),
        P(None, "idx"),
        P(),
        P(None, "idx"),
        P(),
        P(("rep", "idx"), None),
        P(("rep", "idx"), None),
        P(("rep", "idx"), None),
    )
    return jax.shard_map(
        local,
        mesh=mesh,
        in_specs=placed,
        out_specs=(P(("rep", "idx"), None), P(("rep", "idx"), None, None)),
        check_vma=False,
    )
```

```python
import math
import jax
import jax.numpy as jnp
from jax import lax
from jax.experimental import pallas as pl
from jax.experimental.pallas import tpu as pltpu
from jax.sharding import PartitionSpec as P

HEADS = 16
PATCHES = 257
CBLK = 8
CAPT = 128
F32 = jnp.float32
BF16 = jnp.bfloat16
VMEM = pltpu.VMEM
VLIMIT = 60 * 1024 * 1024


def dequant_rows(stored, exponents):
    row_count, col_count = stored.shape
    block_count = exponents.shape[0]
    turned = stored.T.astype(F32).reshape(col_count, block_count, row_count // block_count)
    scaled = turned * jnp.exp2(exponents.astype(F32)).T[:, :, None]
    return scaled.reshape(col_count, row_count).astype(BF16)


def layer_norm(token_rows, norm_gain):
    values = token_rows.astype(F32)
    centered = values - jnp.mean(values, axis=-1, keepdims=True)
    inv_scale = lax.rsqrt(jnp.mean(centered * centered, axis=-1, keepdims=True) + 1e-06)
    return (centered * inv_scale * norm_gain).astype(BF16)


def dot_nt(left, right):
    return lax.dot_general(left, right, (((1,), (1,)), ((), ())), preferred_element_type=F32)


MESH = pl.DeviceIdType.MESH
SHARE = 11


def gather_kernel(q_own, p_own, q_out, p_out, q_hold, p_hold, rz, ry, rx, rc, sz, sy, sx, sc, held):
    peers = q_out.shape[0]
    nz = peers // 4
    me = lax.axis_index("idx")
    x = lax.axis_index("rep")
    z, y, c = me // 4, (me // 2) % 2, me % 2
    own, out = (q_own, p_own), (q_out, p_out)

    def at(zz, yy, cc):
        return (zz * 2 + yy) * 2 + cc

    to_y, to_c, to_x = (x, at(z, 1 - y, c)), (x, at(z, y, 1 - c)), (1 - x, me)
    to_up, to_down = (x, me + 4), (x, me - 4)

    barrier = pltpu.get_barrier_semaphore()

    def greet(target):
        pl.semaphore_signal(barrier, inc=1, device_id=target, device_id_type=MESH)

    for target in (to_y, to_c, to_x):
        greet(target)

    @pl.when(z + 1 < nz)
    def _():
        greet(to_up)

    @pl.when(z > 0)
    def _():
        greet(to_down)

    greeted = 3 + jnp.where(z + 1 < nz, 1, 0) + jnp.where(z > 0, 1, 0)
    pl.semaphore_wait(barrier, greeted)

    def rows(a, k):
        unit = own[a].shape[0] // SHARE
        if k == 0:
            return pl.ds(0, 3 * unit)
        if k == 3:
            return pl.ds(0, SHARE * unit)
        side = x if k == 1 else 1 - x
        return pl.ds(pl.multiple_of((3 + 4 * side) * unit, 8), 4 * unit)

    def copy(a, shard, k, mine, send, recv, target):
        span = rows(a, k)
        return pltpu.make_async_remote_copy(
            src_ref=own[a].at[span] if mine else out[a].at[shard, span],
            dst_ref=out[a].at[shard, span],
            send_sem=send,
            recv_sem=recv,
            device_id=target,
            device_id_type=MESH,
        )

    def pos(zz, yy):
        return zz * 2 + yy

    def up(a, zz, k, mine=False):
        return copy(a, at(zz, y, c), k, mine, sz.at[0, a, zz, k], rz.at[a, zz, k], to_up)

    def down(a, zz, k, mine=False):
        return copy(a, at(zz, y, c), k, mine, sz.at[1, a, zz, k], rz.at[a, zz, k], to_down)

    def across(a, zz, k, yy, mine=False):
        return copy(a, at(zz, yy, c), k, mine, sy.at[a, zz, k], ry.at[a, zz, k], to_y)

    def plane(a, zz, yy, k):
        return copy(a, at(zz, yy, c), k, False, sx.at[a, pos(zz, yy)], rx.at[a, pos(zz, yy)], to_x)

    def core(a, zz, yy, cc, k, mine=False):
        slot = 0 if k == 3 else k
        return copy(
            a, at(zz, yy, cc), k, mine, sc.at[a, pos(zz, yy), slot], rc.at[a, pos(zz, yy), slot], to_c
        )

    def each(distance, body):
        if distance == 0:
            body(z, 0)
            return

        @pl.when(z - distance >= 0)
        def _():
            body(z - distance, -1)

        @pl.when(z + distance < nz)
        def _():
            body(z + distance, 1)

    holds = []
    for a in range(2):
        for k in (1, 0):

            @pl.when(z + 1 < nz)
            def _():
                up(a, z, k, True).start()

            @pl.when(z > 0)
            def _():
                down(a, z, k, True).start()

            across(a, z, k, y, True).start()
        core(a, z, y, c, 3, True).start()
        hold = (q_hold, p_hold)[a]
        load = pltpu.make_async_copy(own[a], hold, held.at[a, 0])
        load.start()
        holds.append((load, pltpu.make_async_copy(hold, out[a].at[me], held.at[a, 1])))
    for load, store in holds:
        load.wait()
        store.start()

    for a in range(2):
        for step in range(1, nz + 2):
            if step < nz:

                def from_chain(zz, side):
                    for k in (1, 0):
                        up(a, zz, k).wait_recv()
                        if side < 0:

                            @pl.when(z + 1 < nz)
                            def _():
                                up(a, zz, k).start()
                        else:

                            @pl.when(z > 0)
                            def _():
                                down(a, zz, k).start()

                        across(a, zz, k, y).start()
                        if k == 1:
                            plane(a, zz, y, 1).start()
                        core(a, zz, y, c, k).start()

                each(step, from_chain)
            if step <= nz:

                def from_across(zz, side):
                    for k in (1, 0):
                        across(a, zz, k, 1 - y).wait_recv()
                        if k == 1:
                            plane(a, zz, 1 - y, 1).start()
                        core(a, zz, 1 - y, c, k).start()

                each(step - 1, from_across)
            if step >= 2:

                def from_plane(zz, side):
                    if side != 0:
                        plane(a, zz, y, 2).wait_recv()
                        core(a, zz, y, c, 2).start()
                    plane(a, zz, 1 - y, 2).wait_recv()
                    core(a, zz, 1 - y, c, 2).start()

                each(step - 2, from_plane)

    for a in range(2):
        for distance in range(nz):

            def finish(zz, side):
                first = side == 0
                for k in (1, 0):
                    if side <= 0:

                        @pl.when(z + 1 < nz)
                        def _():
                            up(a, zz, k, first).wait_send()

                    if side >= 0:

                        @pl.when(z > 0)
                        def _():
                            down(a, zz, k, first).wait_send()

                    across(a, zz, k, y, first).wait_send()
                for yy, mine in ((y, first), (1 - y, False)):
                    if mine:
                        core(a, zz, yy, c, 3, True).wait_send()
                        core(a, zz, yy, 1 - c, 3).wait_recv()
                        continue
                    plane(a, zz, yy, 1).wait_send()
                    for k in (1, 0, 2):
                        core(a, zz, yy, c, k).wait_send()
                        core(a, zz, yy, 1 - c, k).wait_recv()

            each(distance, finish)
    for load, store in holds:
        store.wait()


def gather_call(q_own, p_own, peers):
    anywhere = pl.BlockSpec(memory_space=pl.ANY)
    nz = peers // 4
    dma = pltpu.SemaphoreType.DMA
    return pl.pallas_call(
        gather_kernel,
        in_specs=[anywhere] * 2,
        out_specs=(anywhere, anywhere),
        out_shape=tuple(jax.ShapeDtypeStruct((peers,) + own.shape, own.dtype) for own in (q_own, p_own)),
        scratch_shapes=[
            pltpu.VMEM(q_own.shape, q_own.dtype),
            pltpu.VMEM(p_own.shape, p_own.dtype),
            dma((2, nz, 2)),
            dma((2, nz, 2)),
            dma((2, 2 * nz)),
            dma((2, 2 * nz, 3)),
            dma((2, 2, nz, 2)),
            dma((2, nz, 2)),
            dma((2, 2 * nz)),
            dma((2, 2 * nz, 3)),
            dma((2, 2)),
        ],
        compiler_params=pltpu.CompilerParams(
            collective_id=0, has_side_effects=True, vmem_limit_bytes=4 * 1024 * 1024
        ),
        name="gather_weights",
    )(q_own, p_own)


def gather_rows(q_own, p_own, peers, reps):
    fits = all(own.shape[0] % (8 * SHARE) == 0 for own in (q_own, p_own))
    if fits and peers % 8 == 0 and reps == 2:
        w_qkv, w_proj = gather_call(q_own, p_own, peers)
        return tuple(w.reshape(-1, w.shape[2]) for w in (w_qkv, w_proj))
    return tuple(lax.all_gather(own, "idx", axis=0, tiled=True) for own in (q_own, p_own))


def qkv_kernel(images_ref, gain_ref, w_ref, out_ref, normed):
    group, unit, head_dim = out_ref.shape[0], out_ref.shape[1], out_ref.shape[2]

    @pl.when(pl.program_id(0) == 0)
    def _():
        for g in range(group):
            normed[g] = layer_norm(images_ref[g], gain_ref[...])

    for g in range(group):
        rows = dot_nt(w_ref[...], normed[g])
        out_ref[g] = rows.reshape(unit, head_dim, rows.shape[1]).astype(BF16)


def qkv_call(images3, gain, w_rows):
    group, patches, width = images3.shape
    head_dim = width // HEADS
    units = w_rows.shape[0] // head_dim
    step = 4
    return pl.pallas_call(
        qkv_kernel,
        grid=(units // step,),
        in_specs=[
            pl.BlockSpec((group, patches, width), lambda i: (0, 0, 0)),
            pl.BlockSpec((1, width), lambda i: (0, 0)),
            pl.BlockSpec((step * head_dim, width), lambda i: (i, 0)),
        ],
        out_specs=pl.BlockSpec((group, step, head_dim, patches), lambda i: (0, i, 0, 0)),
        out_shape=jax.ShapeDtypeStruct((group, units, head_dim, patches), BF16),
        scratch_shapes=[pltpu.VMEM((group, patches, width), BF16)],
        compiler_params=pltpu.CompilerParams(vmem_limit_bytes=VLIMIT),
        name="qkv",
    )(images3, gain, w_rows)


def attend_kernel(qkv_ref, proj_ref, images_ref, slot_ref, emb_ref, send_ref, mixed):
    group, units, head_dim, patches = qkv_ref.shape
    width = HEADS * head_dim
    scale = head_dim ** (-0.5)
    for g in range(group):

        @pl.loop(0, HEADS)
        def _(h):
            queries, keys, vals = qkv_ref[g, h], qkv_ref[g, HEADS + h], qkv_ref[g, 2 * HEADS + h]
            logits = lax.dot_general(
                keys, queries, (((0,), (0,)), ((), ())), preferred_element_type=F32
            )
            logits = logits * scale
            weights = jnp.exp(logits - jnp.max(logits, axis=0, keepdims=True))
            probs = weights * (1.0 / jnp.sum(weights, axis=0, keepdims=True))
            out = jnp.dot(vals, probs.astype(BF16), preferred_element_type=F32)
            mixed[pl.ds(pl.multiple_of(h * head_dim, 8), head_dim), :] = out

        left = mixed[...].T.astype(BF16)
        hidden = images_ref[g].astype(F32) + dot_nt(left, proj_ref[...])
        inv_scale = lax.rsqrt(jnp.mean(hidden * hidden, axis=-1, keepdims=True) + 1e-06)
        emb_ref[g * patches:(g + 1) * patches, :] = (hidden * inv_scale).astype(BF16)
    slots = math.prod(send_ref.shape[:-1])
    tokens = group * patches
    pick = lax.broadcasted_iota(jnp.int32, (slots, tokens), 0) == slot_ref[...]
    onehot = jnp.where(pick, 1.0, 0.0).astype(BF16)
    sent = jnp.dot(onehot, emb_ref[...], preferred_element_type=F32).astype(BF16)
    if len(send_ref.shape) == 2:
        send_ref[...] = sent
        return
    peers, capacity = send_ref.shape[0], send_ref.shape[1]
    for p in range(peers):
        send_ref[p] = sent[p * capacity:(p + 1) * capacity]


def attend_call(qkv, w_proj, images3, slot_row, slot_shape):
    group, patches, width = images3.shape
    full = pl.BlockSpec(memory_space=VMEM)
    return pl.pallas_call(
        attend_kernel,
        in_specs=[full] * 4,
        out_specs=(full, full),
        out_shape=(
            jax.ShapeDtypeStruct((group * patches, width), BF16),
            jax.ShapeDtypeStruct(slot_shape + (width,), BF16),
        ),
        scratch_shapes=[pltpu.VMEM((width, patches), F32)],
        compiler_params=pltpu.CompilerParams(vmem_limit_bytes=VLIMIT),
        name="attend",
    )(qkv, w_proj, images3, slot_row)


def score_kernel(rows_ref, picks_ref, captions_ref, out_ref):
    every = dot_nt(rows_ref[...], captions_ref[...]).astype(BF16)
    for k in range(picks_ref.shape[1]):
        pick = picks_ref[:, k:k + 1].astype(F32)
        chosen = jnp.zeros((every.shape[0], CAPT), F32)
        for b in range(CBLK):
            block = every[:, b * CAPT:(b + 1) * CAPT].astype(F32)
            chosen = jnp.where(pick == float(b), block, chosen)
        out_ref[:, k * CAPT:(k + 1) * CAPT] = chosen.astype(BF16)


def score_call(rows, picks, captions):
    full = pl.BlockSpec(memory_space=VMEM)
    return pl.pallas_call(
        score_kernel,
        in_specs=[full] * 3,
        out_specs=full,
        out_shape=jax.ShapeDtypeStruct((rows.shape[0], picks.shape[1] * CAPT), BF16),
        compiler_params=pltpu.CompilerParams(vmem_limit_bytes=VLIMIT),
        name="score",
    )(rows, picks, captions)


def stride_of(capacity):
    return -(-capacity // 8) * 8


def exchange_kernel(
    rows_ref, picks_ref, captions_ref, got_ref,
    rows_in, picks_in, flat, every, chosen, rs, rr, ps, pr, bs, br, own_sem,
):
    peers, capacity = rows_ref.shape[0], rows_ref.shape[1]
    stride = flat.shape[0] // peers
    pick_count = chosen.shape[2] // CAPT
    me = lax.axis_index("idx")
    rep = lax.axis_index("rep")

    def other(step):
        return (me + step) % peers

    barrier = pltpu.get_barrier_semaphore()
    for step in range(1, peers):
        pl.semaphore_signal(barrier, inc=1, device_id=(rep, other(step)), device_id_type=MESH)
    pl.semaphore_wait(barrier, peers - 1)

    def send(src, dst, send_sems, recv_sems, step):
        return pltpu.make_async_remote_copy(
            src_ref=src.at[other(step)],
            dst_ref=dst.at[me],
            send_sem=send_sems.at[step],
            recv_sem=recv_sems.at[step],
            device_id=(rep, other(step)),
            device_id_type=MESH,
        )

    order = sorted(range(1, peers), key=lambda step: -min(step, peers - step))
    for step in order:
        send(rows_ref, rows_in, rs, rr, step).start()
    for step in order:
        send(picks_ref, picks_in, ps, pr, step).start()
    own_rows = pltpu.make_async_copy(rows_ref.at[me], rows_in.at[me], own_sem.at[0])
    own_picks = pltpu.make_async_copy(picks_ref.at[me], picks_in.at[me], own_sem.at[1])
    own_rows.start()
    own_picks.start()
    own_rows.wait()
    own_picks.wait()
    for step in order:
        send(rows_ref, rows_in, rs, rr, step).wait()
        send(picks_ref, picks_in, ps, pr, step).wait()
    for p in range(peers):
        flat[p * stride:p * stride + capacity, :] = rows_in[p]
    every[...] = dot_nt(flat[...], captions_ref[...])
    for p in range(peers):
        columns = picks_in[p].astype(F32).T
        span = slice(p * stride, p * stride + capacity)
        for k in range(pick_count):
            pick = columns[:capacity, k:k + 1]
            best = jnp.zeros((capacity, CAPT), F32)
            for b in range(CBLK):
                best = jnp.where(pick == float(b), every[span, b * CAPT:(b + 1) * CAPT], best)
            chosen[p, :, k * CAPT:(k + 1) * CAPT] = best.astype(BF16)
    for step in order:
        send(chosen, got_ref, bs, br, step).start()
    own_back = pltpu.make_async_copy(chosen.at[me], got_ref.at[me], own_sem.at[2])
    own_back.start()
    own_back.wait()
    for step in order:
        send(chosen, got_ref, bs, br, step).wait()


def exchange_call(rows, picks, captions, pick_count):
    peers, capacity, width = rows.shape
    full = pl.BlockSpec(memory_space=VMEM)
    flat = peers * stride_of(capacity)
    dma = pltpu.SemaphoreType.DMA
    return pl.pallas_call(
        exchange_kernel,
        in_specs=[full] * 3,
        out_specs=pl.BlockSpec(memory_space=pl.ANY),
        out_shape=jax.ShapeDtypeStruct((peers, capacity, pick_count * CAPT), BF16),
        scratch_shapes=[
            pltpu.VMEM(rows.shape, BF16),
            pltpu.VMEM(picks.shape, BF16),
            pltpu.VMEM((flat, width), BF16),
            pltpu.VMEM((flat, captions.shape[0]), F32),
            pltpu.VMEM((peers, capacity, pick_count * CAPT), BF16),
        ]
        + [dma((peers,))] * 6
        + [dma((3,))],
        compiler_params=pltpu.CompilerParams(
            collective_id=1, has_side_effects=True, vmem_limit_bytes=VLIMIT
        ),
        name="exchange",
    )(rows, picks, captions)


def return_kernel(slot_ref, rows_ref, out_ref, *packed):
    if packed:
        (flat,) = packed
        flat[...] = jnp.zeros_like(flat)
        stride = flat.shape[0] // rows_ref.shape[0]
        for p in range(rows_ref.shape[0]):
            flat[p * stride:p * stride + rows_ref.shape[1], :] = rows_ref[p]
        rows = flat[...]
    else:
        rows = rows_ref[...]
    tokens, slots = out_ref.shape[0], rows.shape[0]
    pick = lax.broadcasted_iota(jnp.int32, (tokens, slots), 1) == slot_ref[...]
    onehot = jnp.where(pick, 1.0, 0.0).astype(BF16)
    got = jnp.dot(onehot, rows, preferred_element_type=F32).astype(BF16)
    for k in range(out_ref.shape[1]):
        out_ref[:, k, :] = got[:, k * CAPT:(k + 1) * CAPT]


def return_call(slot_col, rows, pick_count):
    full = pl.BlockSpec(memory_space=VMEM)
    return pl.pallas_call(
        return_kernel,
        in_specs=[full] * 2,
        out_specs=full,
        out_shape=jax.ShapeDtypeStruct((slot_col.shape[0], pick_count, CAPT), BF16),
        scratch_shapes=[pltpu.VMEM((rows.shape[0] * stride_of(rows.shape[1]), rows.shape[2]), BF16)]
        if rows.ndim == 3
        else [],
        compiler_params=pltpu.CompilerParams(vmem_limit_bytes=VLIMIT),
        name="give_back",
    )(slot_col, rows)


def local(
    images,
    norm_gain,
    qkv_values,
    qkv_exponents,
    proj_values,
    proj_exponents,
    captions,
    owners,
    candidates,
):
    token_count, width = images.shape
    peer_count = lax.axis_size("idx")
    me = lax.axis_index("idx")
    capacity = (token_count + peer_count - 1) // peer_count + 1

    def own_exponents(exponents, cols):
        return lax.dynamic_slice_in_dim(exponents, me * cols, cols, axis=1)

    qkv_cols, proj_cols = qkv_values.shape[1], proj_values.shape[1]
    qkv_own = dequant_rows(qkv_values, own_exponents(qkv_exponents, qkv_cols))
    proj_own = dequant_rows(proj_values, own_exponents(proj_exponents, proj_cols))
    w_qkv, w_proj = gather_rows(qkv_own, proj_own, peer_count, lax.axis_size("rep"))

    owner_ids = owners[:, 0]
    onehot = (owner_ids[:, None] == jnp.arange(peer_count, dtype=jnp.int32)[None, :]).astype(
        jnp.int32
    )
    slot_rank = jnp.sum((jnp.cumsum(onehot, axis=0) - onehot) * onehot, axis=1)
    slot_index = owner_ids * capacity + slot_rank
    slots = peer_count * capacity
    pick_count = candidates.shape[1]
    dispatch = (jnp.arange(slots, dtype=jnp.int32)[:, None] == slot_index[None, :]).astype(BF16)
    send_picks = jnp.dot(dispatch, candidates.astype(BF16), preferred_element_type=F32).astype(BF16)
    images3 = images.reshape(-1, PATCHES, width)
    qkv = qkv_call(images3, norm_gain[None, :], w_qkv)
    if capacity >= 16:
        turned = send_picks.reshape(peer_count, capacity, pick_count).transpose(0, 2, 1)
        turned = jnp.pad(turned, ((0, 0), (0, 16 - pick_count), (0, 128 - capacity)))
        embedding, send_rows = attend_call(
            qkv, w_proj, images3, slot_index[None, :], (peer_count, capacity)
        )
        returned = exchange_call(send_rows, turned, captions, pick_count)
        place = owner_ids * stride_of(capacity) + slot_rank
    else:
        embedding, send_rows = attend_call(qkv, w_proj, images3, slot_index[None, :], (slots,))

        def swap(blocks):
            shaped = blocks.reshape(peer_count, capacity, blocks.shape[1])
            moved = lax.all_to_all(shaped, "idx", split_axis=0, concat_axis=0, tiled=True)
            return moved.reshape(blocks.shape)

        returned = swap(score_call(swap(send_rows), swap(send_picks), captions))
        place = slot_index
    scores = return_call(place[:, None], returned, pick_count)
    return (embedding, scores)


def solution(mesh):
    placed = (
        P(("rep", "idx"), None),
        P(),
        P(None, "idx"),
        P(),
        P(None, "idx"),
        P(),
        P(("rep", "idx"), None),
        P(("rep", "idx"), None),
        P(("rep", "idx"), None),
    )
    return jax.shard_map(
        local,
        mesh=mesh,
        in_specs=placed,
        out_specs=(P(("rep", "idx"), None), P(("rep", "idx"), None, None)),
        check_vma=False,
    )
```

```python
import math
import jax
import jax.numpy as jnp
from jax import lax
from jax.experimental import pallas as pl
from jax.experimental.pallas import tpu as pltpu
from jax.sharding import PartitionSpec as P

HEADS = 16
PATCHES = 257
CBLK = 8
CAPT = 128
F32 = jnp.float32
BF16 = jnp.bfloat16
VMEM = pltpu.VMEM
VLIMIT = 60 * 1024 * 1024


def dequant_rows(stored, exponents):
    row_count, col_count = stored.shape
    block_count = exponents.shape[0]
    turned = stored.T.astype(F32).reshape(col_count, block_count, row_count // block_count)
    scaled = turned * jnp.exp2(exponents.astype(F32)).T[:, :, None]
    return scaled.reshape(col_count, row_count).astype(BF16)


def layer_norm(token_rows, norm_gain):
    values = token_rows.astype(F32)
    centered = values - jnp.mean(values, axis=-1, keepdims=True)
    inv_scale = lax.rsqrt(jnp.mean(centered * centered, axis=-1, keepdims=True) + 1e-06)
    return (centered * inv_scale * norm_gain).astype(BF16)


def dot_nt(left, right):
    return lax.dot_general(left, right, (((1,), (1,)), ((), ())), preferred_element_type=F32)


MESH = pl.DeviceIdType.MESH
SHARE = 11


def gather_kernel(q_own, p_own, q_out, p_out, q_hold, p_hold, rz, ry, rx, rc, sz, sy, sx, sc, held):
    peers = q_out.shape[0]
    nz = peers // 4
    me = lax.axis_index("idx")
    x = lax.axis_index("rep")
    z, y, c = me // 4, (me // 2) % 2, me % 2
    own, out = (q_own, p_own), (q_out, p_out)

    def at(zz, yy, cc):
        return (zz * 2 + yy) * 2 + cc

    to_y, to_c, to_x = (x, at(z, 1 - y, c)), (x, at(z, y, 1 - c)), (1 - x, me)
    to_up, to_down = (x, me + 4), (x, me - 4)

    barrier = pltpu.get_barrier_semaphore()

    def greet(target):
        pl.semaphore_signal(barrier, inc=1, device_id=target, device_id_type=MESH)

    for target in (to_y, to_c, to_x):
        greet(target)

    @pl.when(z + 1 < nz)
    def _():
        greet(to_up)

    @pl.when(z > 0)
    def _():
        greet(to_down)

    greeted = 3 + jnp.where(z + 1 < nz, 1, 0) + jnp.where(z > 0, 1, 0)
    pl.semaphore_wait(barrier, greeted)

    def rows(a, k):
        unit = own[a].shape[0] // SHARE
        if k == 0:
            return pl.ds(0, 3 * unit)
        if k == 3:
            return pl.ds(0, SHARE * unit)
        side = x if k == 1 else 1 - x
        return pl.ds(pl.multiple_of((3 + 4 * side) * unit, 8), 4 * unit)

    def copy(a, shard, k, mine, send, recv, target):
        span = rows(a, k)
        return pltpu.make_async_remote_copy(
            src_ref=own[a].at[span] if mine else out[a].at[shard, span],
            dst_ref=out[a].at[shard, span],
            send_sem=send,
            recv_sem=recv,
            device_id=target,
            device_id_type=MESH,
        )

    def pos(zz, yy):
        return zz * 2 + yy

    def up(a, zz, k, mine=False):
        return copy(a, at(zz, y, c), k, mine, sz.at[0, a, zz, k], rz.at[a, zz, k], to_up)

    def down(a, zz, k, mine=False):
        return copy(a, at(zz, y, c), k, mine, sz.at[1, a, zz, k], rz.at[a, zz, k], to_down)

    def across(a, zz, k, yy, mine=False):
        return copy(a, at(zz, yy, c), k, mine, sy.at[a, zz, k], ry.at[a, zz, k], to_y)

    def plane(a, zz, yy, k):
        return copy(a, at(zz, yy, c), k, False, sx.at[a, pos(zz, yy)], rx.at[a, pos(zz, yy)], to_x)

    def core(a, zz, yy, cc, k, mine=False):
        slot = 0 if k == 3 else k
        return copy(
            a, at(zz, yy, cc), k, mine, sc.at[a, pos(zz, yy), slot], rc.at[a, pos(zz, yy), slot], to_c
        )

    def each(distance, body):
        if distance == 0:
            body(z, 0)
            return

        @pl.when(z - distance >= 0)
        def _():
            body(z - distance, -1)

        @pl.when(z + distance < nz)
        def _():
            body(z + distance, 1)

    holds = []
    for a in range(2):
        for k in (1, 0):

            @pl.when(z + 1 < nz)
            def _():
                up(a, z, k, True).start()

            @pl.when(z > 0)
            def _():
                down(a, z, k, True).start()

            across(a, z, k, y, True).start()
        core(a, z, y, c, 3, True).start()
        hold = (q_hold, p_hold)[a]
        load = pltpu.make_async_copy(own[a], hold, held.at[a, 0])
        load.start()
        holds.append((load, pltpu.make_async_copy(hold, out[a].at[me], held.at[a, 1])))
    for load, store in holds:
        load.wait()
        store.start()

    for a in range(2):
        for step in range(1, nz + 2):
            if step < nz:

                def from_chain(zz, side):
                    for k in (1, 0):
                        up(a, zz, k).wait_recv()
                        if side < 0:

                            @pl.when(z + 1 < nz)
                            def _():
                                up(a, zz, k).start()
                        else:

                            @pl.when(z > 0)
                            def _():
                                down(a, zz, k).start()

                        across(a, zz, k, y).start()
                        if k == 1:
                            plane(a, zz, y, 1).start()
                        core(a, zz, y, c, k).start()

                each(step, from_chain)
            if step <= nz:

                def from_across(zz, side):
                    for k in (1, 0):
                        across(a, zz, k, 1 - y).wait_recv()
                        if k == 1:
                            plane(a, zz, 1 - y, 1).start()
                        core(a, zz, 1 - y, c, k).start()

                each(step - 1, from_across)
            if step >= 2:

                def from_plane(zz, side):
                    if side != 0:
                        plane(a, zz, y, 2).wait_recv()
                        core(a, zz, y, c, 2).start()
                    plane(a, zz, 1 - y, 2).wait_recv()
                    core(a, zz, 1 - y, c, 2).start()

                each(step - 2, from_plane)

    for a in range(2):
        for distance in range(nz):

            def finish(zz, side):
                first = side == 0
                for k in (1, 0):
                    if side <= 0:

                        @pl.when(z + 1 < nz)
                        def _():
                            up(a, zz, k, first).wait_send()

                    if side >= 0:

                        @pl.when(z > 0)
                        def _():
                            down(a, zz, k, first).wait_send()

                    across(a, zz, k, y, first).wait_send()
                for yy, mine in ((y, first), (1 - y, False)):
                    if mine:
                        core(a, zz, yy, c, 3, True).wait_send()
                        core(a, zz, yy, 1 - c, 3).wait_recv()
                        continue
                    plane(a, zz, yy, 1).wait_send()
                    for k in (1, 0, 2):
                        core(a, zz, yy, c, k).wait_send()
                        core(a, zz, yy, 1 - c, k).wait_recv()

            each(distance, finish)
    for load, store in holds:
        store.wait()


def gather_call(q_own, p_own, peers):
    anywhere = pl.BlockSpec(memory_space=pl.ANY)
    nz = peers // 4
    dma = pltpu.SemaphoreType.DMA
    return pl.pallas_call(
        gather_kernel,
        in_specs=[anywhere] * 2,
        out_specs=(anywhere, anywhere),
        out_shape=tuple(jax.ShapeDtypeStruct((peers,) + own.shape, own.dtype) for own in (q_own, p_own)),
        scratch_shapes=[
            pltpu.VMEM(q_own.shape, q_own.dtype),
            pltpu.VMEM(p_own.shape, p_own.dtype),
            dma((2, nz, 2)),
            dma((2, nz, 2)),
            dma((2, 2 * nz)),
            dma((2, 2 * nz, 3)),
            dma((2, 2, nz, 2)),
            dma((2, nz, 2)),
            dma((2, 2 * nz)),
            dma((2, 2 * nz, 3)),
            dma((2, 2)),
        ],
        compiler_params=pltpu.CompilerParams(
            collective_id=0, has_side_effects=True, vmem_limit_bytes=4 * 1024 * 1024
        ),
        name="gather_weights",
    )(q_own, p_own)


def gather_rows(q_own, p_own, peers, reps):
    fits = all(own.shape[0] % (8 * SHARE) == 0 for own in (q_own, p_own))
    if fits and peers % 8 == 0 and reps == 2:
        w_qkv, w_proj = gather_call(q_own, p_own, peers)
        return tuple(w.reshape(-1, w.shape[2]) for w in (w_qkv, w_proj))
    return tuple(lax.all_gather(own, "idx", axis=0, tiled=True) for own in (q_own, p_own))


def qkv_kernel(images_ref, gain_ref, w_ref, out_ref, normed):
    group, unit, head_dim = out_ref.shape[0], out_ref.shape[1], out_ref.shape[2]

    @pl.when(pl.program_id(0) == 0)
    def _():
        normed[...] = layer_norm(images_ref[...], gain_ref[...])

    patches = out_ref.shape[3]
    every = dot_nt(w_ref[...], normed[...])
    for g in range(group):
        rows = every[:, g * patches:(g + 1) * patches]
        out_ref[g] = rows.reshape(unit, head_dim, patches).astype(BF16)


def qkv_call(images, gain, w_rows):
    tokens, width = images.shape
    patches = PATCHES
    group = tokens // patches
    head_dim = width // HEADS
    units = w_rows.shape[0] // head_dim
    step = 4
    return pl.pallas_call(
        qkv_kernel,
        grid=(units // step,),
        in_specs=[
            pl.BlockSpec((tokens, width), lambda i: (0, 0)),
            pl.BlockSpec((1, width), lambda i: (0, 0)),
            pl.BlockSpec((step * head_dim, width), lambda i: (i, 0)),
        ],
        out_specs=pl.BlockSpec((group, step, head_dim, patches), lambda i: (0, i, 0, 0)),
        out_shape=jax.ShapeDtypeStruct((group, units, head_dim, patches), BF16),
        scratch_shapes=[pltpu.VMEM((tokens, width), BF16)],
        compiler_params=pltpu.CompilerParams(vmem_limit_bytes=VLIMIT),
        name="qkv",
    )(images, gain, w_rows)


def attend_kernel(qkv_ref, proj_ref, images_ref, slot_ref, emb_ref, send_ref, mixed):
    group, units, head_dim, patches = qkv_ref.shape
    width = HEADS * head_dim
    scale = head_dim ** (-0.5)
    for g in range(group):

        @pl.loop(0, HEADS, unroll=4)
        def _(h):
            queries, keys, vals = qkv_ref[g, h], qkv_ref[g, HEADS + h], qkv_ref[g, 2 * HEADS + h]
            logits = lax.dot_general(
                keys, queries, (((0,), (0,)), ((), ())), preferred_element_type=F32
            )
            logits = logits * scale
            weights = jnp.exp(logits - jnp.max(logits, axis=0, keepdims=True))
            probs = weights * (1.0 / jnp.sum(weights, axis=0, keepdims=True))
            out = jnp.dot(vals, probs.astype(BF16), preferred_element_type=F32)
            mixed[pl.ds(pl.multiple_of(h * head_dim, 8), head_dim), :] = out

        left = mixed[...].T.astype(BF16)
        hidden = images_ref[g * patches:(g + 1) * patches, :].astype(F32) + dot_nt(left, proj_ref[...])
        inv_scale = lax.rsqrt(jnp.mean(hidden * hidden, axis=-1, keepdims=True) + 1e-06)
        emb_ref[g * patches:(g + 1) * patches, :] = (hidden * inv_scale).astype(BF16)
    slots = math.prod(send_ref.shape[:-1])
    tokens = group * patches
    pick = lax.broadcasted_iota(jnp.int32, (slots, tokens), 0) == slot_ref[...]
    onehot = jnp.where(pick, 1.0, 0.0).astype(BF16)
    sent = jnp.dot(onehot, emb_ref[...], preferred_element_type=F32).astype(BF16)
    if len(send_ref.shape) == 2:
        send_ref[...] = sent
        return
    peers, capacity = send_ref.shape[0], send_ref.shape[1]
    for p in range(peers):
        send_ref[p] = sent[p * capacity:(p + 1) * capacity]


def attend_call(qkv, w_proj, images, slot_row, slot_shape):
    tokens, width = images.shape
    patches = qkv.shape[3]
    group = tokens // patches
    full = pl.BlockSpec(memory_space=VMEM)
    return pl.pallas_call(
        attend_kernel,
        in_specs=[full] * 4,
        out_specs=(full, full),
        out_shape=(
            jax.ShapeDtypeStruct((group * patches, width), BF16),
            jax.ShapeDtypeStruct(slot_shape + (width,), BF16),
        ),
        scratch_shapes=[pltpu.VMEM((width, patches), F32)],
        compiler_params=pltpu.CompilerParams(vmem_limit_bytes=VLIMIT),
        name="attend",
    )(qkv, w_proj, images, slot_row)


def score_kernel(rows_ref, picks_ref, captions_ref, out_ref):
    every = dot_nt(rows_ref[...], captions_ref[...]).astype(BF16)
    for k in range(picks_ref.shape[1]):
        pick = picks_ref[:, k:k + 1].astype(F32)
        chosen = jnp.zeros((every.shape[0], CAPT), F32)
        for b in range(CBLK):
            block = every[:, b * CAPT:(b + 1) * CAPT].astype(F32)
            chosen = jnp.where(pick == float(b), block, chosen)
        out_ref[:, k * CAPT:(k + 1) * CAPT] = chosen.astype(BF16)


def score_call(rows, picks, captions):
    full = pl.BlockSpec(memory_space=VMEM)
    return pl.pallas_call(
        score_kernel,
        in_specs=[full] * 3,
        out_specs=full,
        out_shape=jax.ShapeDtypeStruct((rows.shape[0], picks.shape[1] * CAPT), BF16),
        compiler_params=pltpu.CompilerParams(vmem_limit_bytes=VLIMIT),
        name="score",
    )(rows, picks, captions)


def stride_of(capacity):
    return -(-capacity // 8) * 8


def exchange_kernel(
    rows_ref, picks_ref, captions_ref, got_ref,
    rows_in, picks_in, flat, every, chosen, rs, rr, ps, pr, bs, br, own_sem,
):
    peers, capacity = rows_ref.shape[0], rows_ref.shape[1]
    stride = flat.shape[0] // peers
    pick_count = chosen.shape[2] // CAPT
    me = lax.axis_index("idx")
    rep = lax.axis_index("rep")

    def other(step):
        return (me + step) % peers

    barrier = pltpu.get_barrier_semaphore()
    for step in range(1, peers):
        pl.semaphore_signal(barrier, inc=1, device_id=(rep, other(step)), device_id_type=MESH)
    pl.semaphore_wait(barrier, peers - 1)

    def send(src, dst, send_sems, recv_sems, step):
        return pltpu.make_async_remote_copy(
            src_ref=src.at[other(step)],
            dst_ref=dst.at[me],
            send_sem=send_sems.at[step],
            recv_sem=recv_sems.at[step],
            device_id=(rep, other(step)),
            device_id_type=MESH,
        )

    order = sorted(range(1, peers), key=lambda step: -min(step, peers - step))
    for step in order:
        send(rows_ref, rows_in, rs, rr, step).start()
    for step in order:
        send(picks_ref, picks_in, ps, pr, step).start()
    own_rows = pltpu.make_async_copy(rows_ref.at[me], rows_in.at[me], own_sem.at[0])
    own_picks = pltpu.make_async_copy(picks_ref.at[me], picks_in.at[me], own_sem.at[1])
    own_rows.start()
    own_picks.start()
    own_rows.wait()
    own_picks.wait()
    for step in order:
        send(rows_ref, rows_in, rs, rr, step).wait()
        send(picks_ref, picks_in, ps, pr, step).wait()
    for p in range(peers):
        flat[p * stride:p * stride + capacity, :] = rows_in[p]
    every[...] = dot_nt(flat[...], captions_ref[...])
    for p in range(peers):
        columns = picks_in[p].astype(F32).T
        span = slice(p * stride, p * stride + capacity)
        for k in range(pick_count):
            pick = columns[:capacity, k:k + 1]
            best = jnp.zeros((capacity, CAPT), F32)
            for b in range(CBLK):
                best = jnp.where(pick == float(b), every[span, b * CAPT:(b + 1) * CAPT], best)
            chosen[p, :, k * CAPT:(k + 1) * CAPT] = best.astype(BF16)
    for step in order:
        send(chosen, got_ref, bs, br, step).start()
    own_back = pltpu.make_async_copy(chosen.at[me], got_ref.at[me], own_sem.at[2])
    own_back.start()
    own_back.wait()
    for step in order:
        send(chosen, got_ref, bs, br, step).wait()


def exchange_call(rows, picks, captions, pick_count):
    peers, capacity, width = rows.shape
    full = pl.BlockSpec(memory_space=VMEM)
    flat = peers * stride_of(capacity)
    dma = pltpu.SemaphoreType.DMA
    return pl.pallas_call(
        exchange_kernel,
        in_specs=[full] * 3,
        out_specs=pl.BlockSpec(memory_space=pl.ANY),
        out_shape=jax.ShapeDtypeStruct((peers, capacity, pick_count * CAPT), BF16),
        scratch_shapes=[
            pltpu.VMEM(rows.shape, BF16),
            pltpu.VMEM(picks.shape, BF16),
            pltpu.VMEM((flat, width), BF16),
            pltpu.VMEM((flat, captions.shape[0]), F32),
            pltpu.VMEM((peers, capacity, pick_count * CAPT), BF16),
        ]
        + [dma((peers,))] * 6
        + [dma((3,))],
        compiler_params=pltpu.CompilerParams(
            collective_id=1, has_side_effects=True, vmem_limit_bytes=VLIMIT
        ),
        name="exchange",
    )(rows, picks, captions)


def return_kernel(slot_ref, rows_ref, out_ref, *packed):
    if packed:
        (flat,) = packed
        flat[...] = jnp.zeros_like(flat)
        stride = flat.shape[0] // rows_ref.shape[0]
        for p in range(rows_ref.shape[0]):
            flat[p * stride:p * stride + rows_ref.shape[1], :] = rows_ref[p]
        rows = flat[...]
    else:
        rows = rows_ref[...]
    tokens, slots = out_ref.shape[0], rows.shape[0]
    pick = lax.broadcasted_iota(jnp.int32, (tokens, slots), 1) == slot_ref[...]
    onehot = jnp.where(pick, 1.0, 0.0).astype(BF16)
    got = jnp.dot(onehot, rows, preferred_element_type=F32).astype(BF16)
    for k in range(out_ref.shape[1]):
        out_ref[:, k, :] = got[:, k * CAPT:(k + 1) * CAPT]


def return_call(slot_col, rows, pick_count):
    full = pl.BlockSpec(memory_space=VMEM)
    return pl.pallas_call(
        return_kernel,
        in_specs=[full] * 2,
        out_specs=full,
        out_shape=jax.ShapeDtypeStruct((slot_col.shape[0], pick_count, CAPT), BF16),
        scratch_shapes=[pltpu.VMEM((rows.shape[0] * stride_of(rows.shape[1]), rows.shape[2]), BF16)]
        if rows.ndim == 3
        else [],
        compiler_params=pltpu.CompilerParams(vmem_limit_bytes=VLIMIT),
        name="give_back",
    )(slot_col, rows)


def local(
    images,
    norm_gain,
    qkv_values,
    qkv_exponents,
    proj_values,
    proj_exponents,
    captions,
    owners,
    candidates,
):
    token_count, width = images.shape
    peer_count = lax.axis_size("idx")
    me = lax.axis_index("idx")
    capacity = (token_count + peer_count - 1) // peer_count + 1

    def own_exponents(exponents, cols):
        return lax.dynamic_slice_in_dim(exponents, me * cols, cols, axis=1)

    qkv_cols, proj_cols = qkv_values.shape[1], proj_values.shape[1]
    qkv_own = dequant_rows(qkv_values, own_exponents(qkv_exponents, qkv_cols))
    proj_own = dequant_rows(proj_values, own_exponents(proj_exponents, proj_cols))
    w_qkv, w_proj = gather_rows(qkv_own, proj_own, peer_count, lax.axis_size("rep"))

    owner_ids = owners[:, 0]
    onehot = (owner_ids[:, None] == jnp.arange(peer_count, dtype=jnp.int32)[None, :]).astype(
        jnp.int32
    )
    slot_rank = jnp.sum((jnp.cumsum(onehot, axis=0) - onehot) * onehot, axis=1)
    slot_index = owner_ids * capacity + slot_rank
    slots = peer_count * capacity
    pick_count = candidates.shape[1]
    dispatch = (jnp.arange(slots, dtype=jnp.int32)[:, None] == slot_index[None, :]).astype(BF16)
    send_picks = jnp.dot(dispatch, candidates.astype(BF16), preferred_element_type=F32).astype(BF16)
    qkv = qkv_call(images, norm_gain[None, :], w_qkv)
    if capacity >= 16:
        turned = send_picks.reshape(peer_count, capacity, pick_count).transpose(0, 2, 1)
        turned = jnp.pad(turned, ((0, 0), (0, 16 - pick_count), (0, 128 - capacity)))
        embedding, send_rows = attend_call(
            qkv, w_proj, images, slot_index[None, :], (peer_count, capacity)
        )
        returned = exchange_call(send_rows, turned, captions, pick_count)
        place = owner_ids * stride_of(capacity) + slot_rank
    else:
        embedding, send_rows = attend_call(qkv, w_proj, images, slot_index[None, :], (slots,))

        def swap(blocks):
            shaped = blocks.reshape(peer_count, capacity, blocks.shape[1])
            moved = lax.all_to_all(shaped, "idx", split_axis=0, concat_axis=0, tiled=True)
            return moved.reshape(blocks.shape)

        returned = swap(score_call(swap(send_rows), swap(send_picks), captions))
        place = slot_index
    scores = return_call(place[:, None], returned, pick_count)
    return (embedding, scores)


def solution(mesh):
    placed = (
        P(("rep", "idx"), None),
        P(),
        P(None, "idx"),
        P(),
        P(None, "idx"),
        P(),
        P(("rep", "idx"), None),
        P(("rep", "idx"), None),
        P(("rep", "idx"), None),
    )
    return jax.shard_map(
        local,
        mesh=mesh,
        in_specs=placed,
        out_specs=(P(("rep", "idx"), None), P(("rep", "idx"), None, None)),
        check_vma=False,
    )
```
